32 devices in a mesh: wide: 8 (over z, core), narrow: 4 (over y, x).
Axes of the slice: x: 2, y: 2, z: 4, core: 2. Of those that a mesh axis runs over, the one named last changes fastest.
Arguments:
- traction: float32 [3, 64, 49152], P(None, None, ('wide', 'narrow')), may hold values from -6 to 6
- near_kernel: bfloat16 [96, 4, 512, 512], P(('wide', 'narrow')), may hold values from -0.125 to 0.125
- neighbours: int32 [96, 4], P(('wide', 'narrow')), may hold values from 0 to 95, as said below
- far_basis: bfloat16 [5, 49152, 128], P(None, ('wide', 'narrow')), may hold values from -4 to 4
- surface_gap: float32 [3, 49152], P(None, ('wide', 'narrow')), may hold values from -3 to 3
- friction: float32 [49152], P(('wide', 'narrow')), may hold values from 0.2 to 1
- contact_flags: int32 [49152], P(('wide', 'narrow')), may hold values 0 or 1
- cluster_order: int32 [49152], P(('wide', 'narrow')), may hold values from 0 to 49151, as said below
- approach: float32 [3, 64], replicated, may hold values from -1 to 2
Outputs:
- traction_new: float32 [3, 64, 49152], P(None, None, ('wide', 'narrow'))
- residual: float32 [3, 64, 49152], P(None, None, ('wide', 'narrow'))
- step_size: float32 [64], replicated
The draws below stay inside these ranges and needn't reach their ends.
Inputs may be any that keep to these rules, and one draw needn't show every extreme that they name: `neighbours`: entry 0 of row b is b itself; the other 3 entries are distinct blocks other than b, each within 3 blocks of b. `cluster_order`: a permutation of the panels that maps every aligned group of 1536 panels onto itself.
All inputs are finite; a program needn't handle non-finite values. No bound on the sum of `contact_flags` on one device may be relied on, other than what follows from the above.
Results may differ from the reference program's by a relative error of at most 0.0034.
Values may be sent and summed in bfloat16 or wider, within the bound.
A program may use at most 64 MiB of HBM per device.

```python
import math
import jax
import jax.numpy as jnp
from jax import lax

C = 64
R = 128
BS = 512
NEAR = 4
BLK_DEV = 3
PAN_DEV = 1536
NBLK = 96
PANELS = 49152
LEVELS = 5


def draw_neighbours(key, part):
    offsets = jnp.concatenate([jnp.arange(-BLK_DEV, 0), jnp.arange(1, BLK_DEV + 1)]).astype(jnp.int32)
    block_ids = jnp.arange(NBLK, dtype=jnp.int32)
    targets = block_ids[:, None] + offsets[None, :]
    valid = (targets >= 0) & (targets < NBLK)
    scores = jax.random.randint(jax.random.fold_in(key, 11), (NBLK, 2 * BLK_DEV), 0, 1 << 16) * (2 * BLK_DEV)
    scores = scores + jnp.arange(2 * BLK_DEV, dtype=jnp.int32)[None, :]
    scores = jnp.where(valid, scores, -1)
    ranked = lax.top_k(scores, NEAR - 1)[1]
    others = jnp.take_along_axis(targets, ranked, axis=1)
    return jnp.concatenate([block_ids[:, None], others], axis=1).astype(jnp.int32)


def draw_cluster_order(key, part):
    groups = PANELS // PAN_DEV
    scores = jax.random.randint(jax.random.fold_in(key, 23), (groups, PAN_DEV), 0, 1 << 16) * PAN_DEV
    scores = scores + jnp.arange(PAN_DEV, dtype=jnp.int32)[None, :]
    shuffled = jnp.argsort(scores, axis=1).astype(jnp.int32)
    offsets = jnp.arange(groups, dtype=jnp.int32)[:, None] * PAN_DEV
    return (shuffled + offsets).reshape(PANELS).astype(jnp.int32)


def place_ends(array, stream_key, low, high):
    extent = array.shape
    place = [jax.random.randint(jax.random.fold_in(stream_key, axis), (), 0, extent[axis]) for axis in range(len(extent))]
    array = array.at[tuple(place)].set(low)
    longest = extent.index(max(extent))
    place[longest] = (place[longest] + 1) % extent[longest]
    return array.at[tuple(place)].set(high)


def levels(own_key, dims, split, smallest, high):
    level, own = 1.0, jax.random.fold_in(own_key, 6)
    for position, parts in split:
        draws = jnp.exp(jax.random.uniform(jax.random.fold_in(own, position), (parts,), jnp.float32, smallest / len(split), high / len(split)))
        level = level * jnp.repeat(draws, dims[position] // parts).reshape([-1 if axis == position else 1 for axis in range(len(dims))])
    return level


def noise(rng, shape, deviation, reach, split=(), kind=jnp.bfloat16):
    factor_of = levels(rng, shape, split, -0.22, 0.18) if split else 1.0
    drawn = jax.random.normal(rng, shape, jnp.float32) * deviation * factor_of
    return jnp.minimum(jnp.maximum(drawn, -reach), reach).astype(kind)


def setup_inputs(seed: int = 0) -> dict:
    splits = jax.random.split(jax.random.key(seed), 10)
    return {
        "traction": noise(splits[0], (3, C, PANELS), 1.0, 6.0, ((2, 32),), jnp.float32),
        "near_kernel": noise(splits[1], (NBLK, NEAR, BS, BS), (NEAR * BS) ** -0.5, 0.125, ((0, 32),)),
        "neighbours": draw_neighbours(jax.random.fold_in(splits[9], 71), 0),
        "far_basis": noise(splits[3], (LEVELS, PANELS, R), 1.0, 4.0, ((1, 32),)),
        "surface_gap": noise(splits[4], (3, PANELS), 0.5, 3.0, ((1, 32),), jnp.float32),
        "friction": jnp.clip(jnp.exp(math.log(1.0) - 1.609438 * jax.random.uniform(splits[5], (PANELS,), jnp.float32) ** levels(splits[5], (PANELS,), ((0, 32),), -0.2, 0.2)), 0.2, 1.0),
        "contact_flags": place_ends((jax.random.randint(splits[6], (PANELS,), 0, 4) < 3).astype(jnp.int32), jax.random.fold_in(splits[6], 1), 0, 1),
        "cluster_order": draw_cluster_order(jax.random.fold_in(splits[9], 71), 0),
        "approach": jnp.clip(jax.random.uniform(splits[8], (3, C), jnp.float32, -1.0, 2.0), -1.0, 2.0),
    }


SLIP_EPS = 0.01

def near_field(field_low, near_kernel, neighbours):
    row_count = field_low.shape[0]
    blocks = field_low.astype(jnp.float32).reshape(row_count, NBLK, BS)

    def one_block(block_id):
        picked = jnp.take(blocks, neighbours[block_id], axis=1)
        weights = near_kernel[block_id].astype(jnp.float32)
        return jnp.einsum('kij,xkj->xi', weights, picked)
    result = lax.map(one_block, jnp.arange(NBLK, dtype=jnp.int32))
    return jnp.transpose(result, (1, 0, 2)).reshape(row_count, PANELS)

def far_field(field_low, far_basis):
    row_count = field_low.shape[0]
    values = field_low.astype(jnp.float32)
    summed = jnp.zeros((row_count, PANELS), jnp.float32)
    for tree_level in range(LEVELS):
        span_len = PAN_DEV * 2 ** (tree_level + 1)
        groups = PANELS // span_len
        factor = far_basis[tree_level].astype(jnp.float32).reshape(groups, span_len, R)
        pieces = values.reshape(row_count, groups, span_len)
        gain = 0.64 / (R * span_len) ** 0.5
        coeffs = (jnp.einsum('xgp,gpr->gxr', pieces, factor) * gain).astype(jnp.bfloat16)
        coeffs = lax.optimization_barrier(coeffs).astype(jnp.float32)
        summed = summed + jnp.einsum('gxr,gpr->xgp', coeffs, factor).reshape(row_count, PANELS)
    return summed

def apply_operator(field, near_kernel, neighbours, far_basis):
    field_low = field.astype(jnp.bfloat16)
    return near_field(field_low, near_kernel, neighbours) + far_field(field_low, far_basis)

def project_cone(trial_point, mu_sorted):
    normal = trial_point[0]
    slide_a = trial_point[1]
    slide_b = trial_point[2]
    slip = jnp.sqrt(slide_a * slide_a + slide_b * slide_b + SLIP_EPS)
    coeff = mu_sorted[None, :]
    stick = slip <= coeff * normal
    pressed = jnp.where(stick, normal, jnp.maximum((normal + coeff * slip) / (1.0 + coeff * coeff), 0.0))
    factor = jnp.where(stick, jnp.ones_like(slip), coeff * pressed / slip)
    return jnp.stack([pressed, factor * slide_a, factor * slide_b])

def reference(traction, near_kernel, neighbours, far_basis, surface_gap, friction, contact_flags, cluster_order, approach):
    gap_sorted = jnp.take(surface_gap, cluster_order, axis=1)
    mu_sorted = jnp.take(friction, cluster_order)
    live_mask = jnp.take(contact_flags, cluster_order).astype(jnp.float32)
    row_count = 3 * C
    state_rows = traction.reshape(row_count, PANELS)
    target = (approach[:, :, None] - gap_sorted[:, None, :]).reshape(row_count, PANELS)
    residual = apply_operator(state_rows, near_kernel, neighbours, far_basis) - target
    image_rows = apply_operator(residual, near_kernel, neighbours, far_basis)
    residual_out = residual.reshape(3, C, PANELS)
    image_out = image_rows.reshape(3, C, PANELS)
    cross_mean = lax.optimization_barrier(jnp.mean(residual_out * image_out, axis=(0, 2)))
    square_mean = lax.optimization_barrier(jnp.mean(image_out * image_out, axis=(0, 2)))
    step_size = cross_mean / (square_mean + 1e-06)
    trial_point = traction - step_size[None, :, None] * residual_out
    updated = project_cone(trial_point, mu_sorted) * live_mask[None, None, :]
    return (updated, residual_out, step_size)
```

```python
import functools
import math

import jax
import jax.numpy as jnp
from jax import lax
from jax.experimental import pallas as pl
from jax.experimental.pallas import tpu as pltpu
from jax.sharding import PartitionSpec as P

SLIP_EPS = 0.01
MESH = pl.DeviceIdType.MESH
GROUP_BITS = 3


def dot(a, b):
    return lax.dot_general(a, b, (((1,), (0,)), ((), ())), preferred_element_type=jnp.float32)


def dot_t(a, b):
    return lax.dot_general(a, b, (((1,), (1,)), ((), ())), preferred_element_type=jnp.float32)


def flip(me, mask):
    peer = me
    bit = 1
    while bit <= mask:
        if mask & bit:
            peer = peer + bit - 2 * bit * ((me // bit) % 2)
        bit *= 2
    return peer


def event_order(chunks, stages):
    step, lead = 6.0, 13.0
    events = []
    for a in range(2):
        for c in range(chunks):
            start = a * lead + c * step
            for s in range(stages):
                events.append((start + 3.0 + 1.8 * s, "tree", a, c, s))
            events.append((start + 5.9, "forward", a, c, 0))
            events.append((start + lead, "finish", a, c, 0))
    return [event[1:] for event in sorted(events, key=lambda event: event[0])]


def kernel(cfg, *refs):
    comps, loads, panels, blocks, near, size, levels, rank, wide, narrow = cfg
    refs = list(refs)
    take = lambda count: [refs.pop(0) for _ in range(count)]
    nb, trac_h, near_h, far_h, gap, fric, flags, order, approach = take(9)
    new_h, res_h, step_ref = take(3)
    trac, kv, bcat, res, table, gs, coef, acc, sums = take(9)
    halos = [take(comps) for _ in range(2)]
    sends, recvs = take(levels), take(levels)
    devices = wide * narrow
    bits = levels
    groups = [(low, min(GROUP_BITS, bits - low)) for low in range(0, bits, GROUP_BITS)]
    slots = take(len(groups))
    load_sem, out_sem, tree_ss, tree_rs, x_ss, x_rs, y_ss, y_rs, stat_ss, stat_rs = take(10)

    me = lax.axis_index("wide") * narrow + lax.axis_index("narrow")
    odd = me % 2
    pair = flip(me, 1)
    onward = me + 2 - 4 * odd
    source = me - 2 + 4 * odd
    has_onward = (onward >= 0) & (onward < devices)
    has_source = (source >= 0) & (source < devices)

    def coords(peer):
        return (peer // narrow, peer % narrow)

    def remote(src, dst, ss, rs, peer):
        return pltpu.make_async_remote_copy(
            src_ref=src, dst_ref=dst, send_sem=ss, recv_sem=rs, device_id=coords(peer), device_id_type=MESH
        )

    trac_in = [pltpu.make_async_copy(trac_h.at[c], trac.at[c], load_sem.at[c]) for c in range(comps)]
    far_in = [
        pltpu.make_async_copy(far_h.at[m], bcat.at[:, m * rank : (m + 1) * rank], load_sem.at[comps + m])
        for m in range(levels)
    ]
    near_in = pltpu.make_async_copy(near_h, kv, load_sem.at[comps + levels])
    for copy in trac_in + far_in:
        copy.start()
    near_in.start()

    masks = set(1 << s for s in range(bits))
    for low, count in groups:
        masks |= set(m << low for m in range(1, 1 << count))
    barrier = pltpu.get_barrier_semaphore()
    for mask in sorted(masks):
        pl.semaphore_signal(barrier, inc=1, device_id=coords(flip(me, mask)), device_id_type=MESH)

    @pl.when(has_onward)
    def _():
        pl.semaphore_signal(barrier, inc=1, device_id=coords(onward), device_id_type=MESH)

    @pl.when(has_source)
    def _():
        pl.semaphore_signal(barrier, inc=1, device_id=coords(source), device_id_type=MESH)

    for a in range(2):
        for c in range(comps):

            @pl.when(me == 0)
            def _():
                halos[a][c][0:blocks] = jnp.zeros((blocks, loads, size), jnp.bfloat16)

            @pl.when(me == devices - 1)
            def _():
                halos[a][c][2 * blocks : 3 * blocks] = jnp.zeros((blocks, loads, size), jnp.bfloat16)

    for c in range(comps):
        trac_in[c].wait()
        for b in range(blocks):
            halos[0][c][blocks + b] = trac[c, :, b * size : (b + 1) * size].astype(jnp.bfloat16)
    for copy in far_in:
        copy.wait()

    def tree_copy(a, c, s):
        return remote(
            sends[s].at[a, c], recvs[s].at[a, c], tree_ss.at[a, c, s], tree_rs.at[a, c, s], flip(me, 1 << s)
        )

    def x_copy(a, c):
        halo = halos[a][c]
        return remote(
            halo.at[pl.ds(blocks, blocks)],
            halo.at[pl.ds((1 - odd) * 0 + odd * 2 * blocks, blocks)],
            x_ss.at[a, c],
            x_rs.at[a, c],
            pair,
        )

    def y_copy(a, c):
        halo = halos[a][c]
        return remote(
            halo.at[pl.ds((1 - odd) * 2 * blocks, blocks)],
            halo.at[pl.ds(odd * 2 * blocks, blocks)],
            y_ss.at[a, c],
            y_rs.at[a, c],
            onward,
        )

    def project(a, c):
        total = dot(halos[a][c][blocks], bcat[0:size, :])
        for b in range(1, blocks):
            total = total + dot(halos[a][c][blocks + b], bcat[b * size : (b + 1) * size, :])
        acc[c] = total
        sends[0][a, c] = total.astype(jnp.bfloat16)

    def launch(a, c):
        tree_copy(a, c, 0).start()
        x_copy(a, c).start()

    for c in range(comps):
        project(0, c)
        if c == 0:
            pl.semaphore_wait(
                barrier, len(masks) + jnp.where(has_onward, 1, 0) + jnp.where(has_source, 1, 0)
            )
        launch(0, c)

    table[...] = jnp.zeros_like(table)
    table[0:comps] = gap[...]
    table[comps : comps + 1] = fric[...]
    table[comps + 1 : comps + 2] = flags[...].astype(jnp.float32)
    whole = table[...]
    high = whole.astype(jnp.bfloat16).astype(jnp.float32)
    rest = whole - high
    middle = rest.astype(jnp.bfloat16).astype(jnp.float32)
    parts = jnp.concatenate([high, middle, rest - middle, jnp.zeros_like(whole)], axis=0).astype(jnp.bfloat16)

    def gather(b, carry):
        cols = pl.ds(pl.multiple_of(b * size, size), size)
        wanted = order[:, cols] - me * panels
        chosen = lax.broadcasted_iota(jnp.int32, (panels, size), 0) == wanted
        picked = dot(parts, chosen.astype(jnp.float32).astype(jnp.bfloat16))
        rows = whole.shape[0]
        gs[:, cols] = picked[0:rows] + picked[rows : 2 * rows] + picked[2 * rows : 3 * rows]
        return carry

    lax.fori_loop(0, blocks, gather, 0)

    diagonal = lax.broadcasted_iota(jnp.int32, (loads, loads), 0) == lax.broadcasted_iota(
        jnp.int32, (loads, loads), 1
    )

    def as_column(row):
        return jnp.sum(jnp.where(diagonal, row, 0.0), axis=1, keepdims=True)

    def as_row(column):
        return jnp.sum(jnp.where(diagonal, column, 0.0), axis=0, keepdims=True)

    columns = [as_column(approach[c : c + 1, :]) for c in range(comps)]
    near_in.wait()

    def tree(a, c, s):
        tree_copy(a, c, s).wait()
        merged = acc[c, :, s * rank :] + recvs[s][a, c].astype(jnp.float32)
        gain = 0.64 / math.sqrt(rank * panels * 2 ** (s + 1))
        coef[c, :, s * rank : (s + 1) * rank] = (merged[:, 0:rank] * gain).astype(jnp.bfloat16)
        if s + 1 < levels:
            acc[c, :, (s + 1) * rank :] = merged[:, rank:]
            sends[s + 1][a, c] = merged[:, rank:].astype(jnp.bfloat16)
            tree_copy(a, c, s + 1).start()

    def forward(a, c):
        x_copy(a, c).wait()

        @pl.when(has_onward)
        def _():
            y_copy(a, c).start()

    def finish(a, c):
        @pl.when(has_source)
        def _():
            y_copy(a, c).wait_recv()

        halo = halos[a][c]

        def block(b, carry):
            cols = pl.ds(pl.multiple_of(b * size, size), size)
            total = dot_t(coef[c], bcat[cols, :])
            for k in range(near):
                slot = nb[b, k] - nb[b, 0] + b + blocks
                total = total + dot_t(halo[slot], kv[b, k])
            if a == 0:
                value = total - (columns[c] - gs[c : c + 1, cols])
                res[c, :, cols] = value
                halos[1][c][blocks + b] = value.astype(jnp.bfloat16)
                return carry
            cross, square = carry
            cross = cross + jnp.sum(res[c, :, cols] * total, axis=1, keepdims=True)
            return cross, square + jnp.sum(total * total, axis=1, keepdims=True)

        if a == 0:
            lax.fori_loop(0, blocks, block, 0)
            project(1, c)
            launch(1, c)
            pltpu.make_async_copy(res.at[c], res_h.at[c], out_sem.at[0, c]).start()
            return None
        zero = jnp.zeros((loads, 1), jnp.float32)
        return lax.fori_loop(0, blocks, block, (zero, zero))

    cross = square = None
    for kind, a, c, s in event_order(comps, levels):
        if kind == "tree":
            tree(a, c, s)
        elif kind == "forward":
            forward(a, c)
        else:
            part = finish(a, c)
            if a == 1:
                cross = part[0] if cross is None else cross + part[0]
                square = part[1] if square is None else square + part[1]

    sums[...] = jnp.zeros_like(sums)
    sums[0:1, 0:loads] = as_row(cross)
    sums[1:2, 0:loads] = as_row(square)
    for g, (low, count) in enumerate(groups):
        slot = slots[g]
        mine = (me // (1 << low)) % (1 << count)
        slot[mine] = sums[...]
        copies = []
        for m in range(1, 1 << count):
            copies.append(
                remote(slot.at[mine], slot.at[mine], stat_ss.at[g, m], stat_rs.at[g, m], flip(me, m << low))
            )
            copies[-1].start()
        for copy in copies:
            copy.wait()
        total = slot[0]
        for m in range(1, 1 << count):
            total = total + slot[m]
        sums[...] = total

    entries = comps * panels * devices
    step_row = sums[0:1, 0:loads] / entries / (sums[1:2, 0:loads] / entries + 1e-06)
    step_ref[...] = step_row
    step = as_column(step_row)

    def update(b, carry):
        cols = pl.ds(pl.multiple_of(b * size, size), size)
        normal = trac[0, :, cols] - step * res[0, :, cols]
        slide_a = trac[1, :, cols] - step * res[1, :, cols]
        slide_b = trac[2, :, cols] - step * res[2, :, cols]
        mu = gs[comps : comps + 1, cols]
        live = gs[comps + 1 : comps + 2, cols]
        slip = jnp.sqrt(slide_a * slide_a + slide_b * slide_b + SLIP_EPS)
        stick = slip <= mu * normal
        pressed = jnp.where(stick, normal, jnp.maximum((normal + mu * slip) / (1.0 + mu * mu), 0.0))
        factor = jnp.where(stick, jnp.ones_like(slip), mu * pressed / slip)
        trac[0, :, cols] = pressed * live
        trac[1, :, cols] = factor * slide_a * live
        trac[2, :, cols] = factor * slide_b * live
        return carry

    lax.fori_loop(0, blocks, update, 0)
    outs = [pltpu.make_async_copy(trac.at[c], new_h.at[c], out_sem.at[1, c]) for c in range(comps)]
    for copy in outs:
        copy.start()
    for a in range(2):
        for c in range(comps):

            @pl.when(has_onward)
            def _():
                y_copy(a, c).wait_send()

    for c in range(comps):
        pltpu.make_async_copy(res.at[c], res_h.at[c], out_sem.at[0, c]).wait()
        outs[c].wait()


def body(wide, narrow, traction, near_kernel, neighbours, far_basis, surface_gap, friction, flags, order, approach):
    comps, loads, panels = traction.shape
    blocks, near, size = near_kernel.shape[:3]
    levels, _, rank = far_basis.shape
    cfg = (comps, loads, panels, blocks, near, size, levels, rank, wide, narrow)
    low = jnp.bfloat16
    groups = [min(GROUP_BITS, levels - at) for at in range(0, levels, GROUP_BITS)]
    dma = pltpu.SemaphoreType.DMA
    vmem = pl.BlockSpec(memory_space=pltpu.VMEM)
    anywhere = pl.BlockSpec(memory_space=pl.ANY)
    scratch = [
        pltpu.VMEM(traction.shape, jnp.float32),
        pltpu.VMEM(near_kernel.shape, low),
        pltpu.VMEM((panels, levels * rank), low),
        pltpu.VMEM(traction.shape, jnp.float32),
        pltpu.VMEM((8, panels), jnp.float32),
        pltpu.VMEM((8, panels), jnp.float32),
        pltpu.VMEM((comps, loads, levels * rank), low),
        pltpu.VMEM((comps, loads, levels * rank), jnp.float32),
        pltpu.VMEM((8, 128), jnp.float32),
    ]
    scratch += [pltpu.VMEM((3 * blocks, loads, size), low) for _ in range(2 * comps)]
    for _ in range(2):
        scratch += [pltpu.VMEM((2, comps, loads, (levels - s) * rank), low) for s in range(levels)]
    scratch += [pltpu.VMEM((1 << count, 8, 128), jnp.float32) for count in groups]
    scratch += [dma((comps + levels + 1,)), dma((2, comps))]
    scratch += [dma((2, comps, levels))] * 2 + [dma((2, comps))] * 4
    scratch += [dma((len(groups), 1 << GROUP_BITS))] * 2
    new, residual, step = pl.pallas_call(
        functools.partial(kernel, cfg),
        out_shape=(
            jax.ShapeDtypeStruct(traction.shape, jnp.float32),
            jax.ShapeDtypeStruct(traction.shape, jnp.float32),
            jax.ShapeDtypeStruct((1, loads), jnp.float32),
        ),
        in_specs=[pl.BlockSpec(memory_space=pltpu.SMEM)] + [anywhere] * 3 + [vmem] * 5,
        out_specs=(anywhere, anywhere, vmem),
        scratch_shapes=scratch,
        compiler_params=pltpu.CompilerParams(
            collective_id=0, has_side_effects=True, vmem_limit_bytes=50 * 1024 * 1024
        ),
    )(
        neighbours,
        traction,
        near_kernel,
        far_basis,
        surface_gap,
        friction.reshape(1, panels),
        flags.reshape(1, panels),
        order.reshape(1, panels),
        approach,
    )
    return new, residual, step.reshape(loads)


def solution(mesh):
    sizes = mesh.shape
    return jax.shard_map(
        functools.partial(body, sizes["wide"], sizes["narrow"]),
        mesh=mesh,
        in_specs=(
            P(None, None, ("wide", "narrow")),
            P(("wide", "narrow"), None, None, None),
            P(("wide", "narrow"), None),
            P(None, ("wide", "narrow"), None),
            P(None, ("wide", "narrow")),
            P(("wide", "narrow")),
            P(("wide", "narrow")),
            P(("wide", "narrow")),
            P(),
        ),
        out_specs=(P(None, None, ("wide", "narrow")), P(None, None, ("wide", "narrow")), P()),
        check_vma=False,
    )
```

```python
import functools
import math

import jax
import jax.numpy as jnp
from jax import lax
from jax.experimental import pallas as pl
from jax.experimental.pallas import tpu as pltpu
from jax.sharding import PartitionSpec as P

SLIP_EPS = 0.01
MESH = pl.DeviceIdType.MESH


def dot(a, b):
    return lax.dot_general(a, b, (((1,), (0,)), ((), ())), preferred_element_type=jnp.float32)


def dot_t(a, b):
    return lax.dot_general(a, b, (((1,), (1,)), ((), ())), preferred_element_type=jnp.float32)


def flip(me, mask):
    peer = me
    bit = 1
    while bit <= mask:
        if mask & bit:
            peer = peer + bit - 2 * bit * ((me // bit) % 2)
        bit *= 2
    return peer


def event_order(chunks, stages):
    step, lead, first, later, ahead = 4.0, 12.0, 2.0, 3.0, 5.0
    events = []
    for a in range(2):
        for c in range(chunks):
            start = a * lead + c * step
            for s in range(stages):
                events.append((start + first + later * s, "tree", a, c, s))
            events.append((start + lead - 0.1, "upper", a, c, 0))
            events.append((start + ahead, "forward", a, c, 0))
            events.append((start + lead, "finish", a, c, 0))
    return [event[1:] for event in sorted(events, key=lambda event: event[0])]


def kernel(cfg, *refs):
    comps, loads, panels, blocks, near, size, levels, rank, wide, narrow = cfg
    refs = list(refs)
    take = lambda count: [refs.pop(0) for _ in range(count)]
    nb, trac_h, near_h, far_h, gap, fric, flags, order, approach = take(9)
    new_h, res_h, step_ref = take(3)
    trac, kv, bcat, res, table, gs, coef, acc, sums = take(9)
    gap_v, fric_v, flags_v, order_v, approach_v = take(5)
    halos = [take(comps) for _ in range(2)]
    devices = wide * narrow
    lower = narrow.bit_length() - 1
    sends, recvs = take(lower + 1), take(lower)
    upper_in = [None] + take(wide - 1)
    groups = [(0, lower), (lower, levels - lower)]
    slots = take(len(groups))
    load_sem, out_sem, tree_ss, tree_rs, up_ss, up_rs, x_ss, x_rs, y_ss, y_rs, stat_ss, stat_rs = take(12)

    me = lax.axis_index("wide") * narrow + lax.axis_index("narrow")
    odd = me % 2
    pair = flip(me, 1)
    onward = me + 2 - 4 * odd
    source = me - 2 + 4 * odd
    has_onward = (onward >= 0) & (onward < devices)
    has_source = (source >= 0) & (source < devices)

    def coords(peer):
        return (peer // narrow, peer % narrow)

    def remote(src, dst, ss, rs, peer):
        return pltpu.make_async_remote_copy(
            src_ref=src, dst_ref=dst, send_sem=ss, recv_sem=rs, device_id=coords(peer), device_id_type=MESH
        )

    trac_in = [pltpu.make_async_copy(trac_h.at[c], trac.at[c], load_sem.at[c]) for c in range(comps)]
    far_in = [
        pltpu.make_async_copy(far_h.at[m], bcat.at[:, m * rank : (m + 1) * rank], load_sem.at[comps + m])
        for m in range(levels)
    ]
    near_in = pltpu.make_async_copy(near_h, kv, load_sem.at[comps + levels])
    small_in = [
        pltpu.make_async_copy(src, dst, load_sem.at[comps + levels + 1 + i])
        for i, (src, dst) in enumerate(
            [(gap, gap_v), (fric, fric_v), (flags, flags_v), (order, order_v), (approach, approach_v)]
        )
    ]
    for copy in trac_in + far_in + small_in:
        copy.start()

    masks = set()
    for low, count in groups:
        masks |= set(m << low for m in range(1, 1 << count))
    barrier = pltpu.get_barrier_semaphore()
    for mask in sorted(masks):
        pl.semaphore_signal(barrier, inc=1, device_id=coords(flip(me, mask)), device_id_type=MESH)

    @pl.when(has_onward)
    def _():
        pl.semaphore_signal(barrier, inc=1, device_id=coords(onward), device_id_type=MESH)

    @pl.when(has_source)
    def _():
        pl.semaphore_signal(barrier, inc=1, device_id=coords(source), device_id_type=MESH)

    for a in range(2):
        for c in range(comps):

            @pl.when(me == 0)
            def _():
                halos[a][c][0:blocks] = jnp.zeros((blocks, loads, size), jnp.bfloat16)

            @pl.when(me == devices - 1)
            def _():
                halos[a][c][2 * blocks : 3 * blocks] = jnp.zeros((blocks, loads, size), jnp.bfloat16)

    for c in range(comps):
        trac_in[c].wait()
        for b in range(blocks):
            halos[0][c][blocks + b] = trac[c, :, b * size : (b + 1) * size].astype(jnp.bfloat16)
    for copy in far_in:
        copy.wait()
    near_in.start()

    def tree_copy(a, c, s):
        return remote(
            sends[s].at[a, c], recvs[s].at[a, c], tree_ss.at[a, c, s], tree_rs.at[a, c, s], flip(me, 1 << s)
        )

    def upper_copy(a, c, m):
        skip = (m.bit_length() - 1) * rank
        return remote(
            sends[lower].at[a, c, :, skip:],
            upper_in[m].at[a, c],
            up_ss.at[a, c, m],
            up_rs.at[a, c, m],
            flip(me, m << lower),
        )

    def x_copy(a, c):
        halo = halos[a][c]
        return remote(
            halo.at[pl.ds(blocks, blocks)],
            halo.at[pl.ds((1 - odd) * 0 + odd * 2 * blocks, blocks)],
            x_ss.at[a, c],
            x_rs.at[a, c],
            pair,
        )

    def y_copy(a, c):
        halo = halos[a][c]
        return remote(
            halo.at[pl.ds((1 - odd) * 2 * blocks, blocks)],
            halo.at[pl.ds(odd * 2 * blocks, blocks)],
            y_ss.at[a, c],
            y_rs.at[a, c],
            onward,
        )

    def project(a, c):
        total = dot(halos[a][c][blocks], bcat[0:size, :])
        for b in range(1, blocks):
            total = total + dot(halos[a][c][blocks + b], bcat[b * size : (b + 1) * size, :])
        acc[c] = total
        sends[0][a, c] = total.astype(jnp.bfloat16)

    def launch(a, c):
        tree_copy(a, c, 0).start()
        x_copy(a, c).start()

    for c in range(comps):
        project(0, c)
        if c == 0:
            pl.semaphore_wait(
                barrier, len(masks) + jnp.where(has_onward, 1, 0) + jnp.where(has_source, 1, 0)
            )
        launch(0, c)

    table[...] = jnp.zeros_like(table)
    for copy in small_in:
        copy.wait()
    table[0:comps] = gap_v[...]
    table[comps : comps + 1] = fric_v[...].reshape(1, panels)
    table[comps + 1 : comps + 2] = flags_v[...].reshape(1, panels).astype(jnp.float32)
    whole = table[...]
    high = whole.astype(jnp.bfloat16).astype(jnp.float32)
    rest = whole - high
    middle = rest.astype(jnp.bfloat16).astype(jnp.float32)
    parts = jnp.concatenate([high, middle, rest - middle, jnp.zeros_like(whole)], axis=0).astype(jnp.bfloat16)

    def gather(b, carry):
        cols = pl.ds(pl.multiple_of(b * size, size), size)
        wanted = order_v[cols].reshape(1, size) - me * panels
        chosen = lax.broadcasted_iota(jnp.int32, (panels, size), 0) == wanted
        picked = dot(parts, chosen.astype(jnp.float32).astype(jnp.bfloat16))
        rows = whole.shape[0]
        gs[:, cols] = picked[0:rows] + picked[rows : 2 * rows] + picked[2 * rows : 3 * rows]
        return carry

    lax.fori_loop(0, blocks, gather, 0)

    diagonal = lax.broadcasted_iota(jnp.int32, (loads, loads), 0) == lax.broadcasted_iota(
        jnp.int32, (loads, loads), 1
    )

    def as_column(row):
        return jnp.sum(jnp.where(diagonal, row, 0.0), axis=1, keepdims=True)

    def as_row(column):
        return jnp.sum(jnp.where(diagonal, column, 0.0), axis=0, keepdims=True)

    columns = [as_column(approach_v[c : c + 1, :]) for c in range(comps)]
    near_in.wait()

    def tree(a, c, s):
        tree_copy(a, c, s).wait()
        merged = acc[c, :, s * rank :] + recvs[s][a, c].astype(jnp.float32)
        gain = 0.64 / math.sqrt(rank * panels * 2 ** (s + 1))
        coef[c, :, s * rank : (s + 1) * rank] = (merged[:, 0:rank] * gain).astype(jnp.bfloat16)
        acc[c, :, (s + 1) * rank :] = merged[:, rank:]
        sends[s + 1][a, c] = merged[:, rank:].astype(jnp.bfloat16)
        if s + 1 < lower:
            tree_copy(a, c, s + 1).start()
        else:
            for m in reversed(range(1, wide)):
                upper_copy(a, c, m).start()

    def upper(a, c):
        total = acc[c, :, lower * rank :]
        for u in range(levels - lower):
            extra = None
            for m in range(1 << u, 2 << u):
                upper_copy(a, c, m).wait()
                piece = upper_in[m][a, c].astype(jnp.float32)
                extra = piece if extra is None else extra + piece
            total = total + extra
            gain = 0.64 / math.sqrt(rank * panels * 2 ** (lower + u + 1))
            at = (lower + u) * rank
            coef[c, :, at : at + rank] = (total[:, 0:rank] * gain).astype(jnp.bfloat16)
            total = total[:, rank:]

    def forward(a, c):
        x_copy(a, c).wait()

        @pl.when(has_onward)
        def _():
            y_copy(a, c).start()

    def finish(a, c):
        @pl.when(has_source)
        def _():
            y_copy(a, c).wait_recv()

        halo = halos[a][c]

        def block(b, carry):
            cols = pl.ds(pl.multiple_of(b * size, size), size)
            total = dot_t(coef[c], bcat[cols, :])
            for k in range(near):
                slot = nb[b, k] - nb[b, 0] + b + blocks
                total = total + dot_t(halo[slot], kv[b, k])
            if a == 0:
                value = total - (columns[c] - gs[c : c + 1, cols])
                res[c, :, cols] = value
                halos[1][c][blocks + b] = value.astype(jnp.bfloat16)
                return carry
            cross, square = carry
            cross = cross + jnp.sum(res[c, :, cols] * total, axis=1, keepdims=True)
            return cross, square + jnp.sum(total * total, axis=1, keepdims=True)

        if a == 0:
            lax.fori_loop(0, blocks, block, 0)
            project(1, c)
            launch(1, c)
            pltpu.make_async_copy(res.at[c], res_h.at[c], out_sem.at[0, c]).start()
            return None
        zero = jnp.zeros((loads, 1), jnp.float32)
        return lax.fori_loop(0, blocks, block, (zero, zero))

    cross = square = None
    for kind, a, c, s in event_order(comps, lower):
        if kind == "tree":
            tree(a, c, s)
        elif kind == "upper":
            upper(a, c)
        elif kind == "forward":
            forward(a, c)
        else:
            part = finish(a, c)
            if a == 1:
                cross = part[0] if cross is None else cross + part[0]
                square = part[1] if square is None else square + part[1]

    sums[...] = jnp.zeros_like(sums)
    sums[0:1, 0:loads] = as_row(cross)
    sums[1:2, 0:loads] = as_row(square)
    for g, (low, count) in enumerate(groups):
        slot = slots[g]
        mine = (me // (1 << low)) % (1 << count)
        slot[mine] = sums[...]
        copies = []
        for m in range(1, 1 << count):
            copies.append(
                remote(slot.at[mine], slot.at[mine], stat_ss.at[g, m], stat_rs.at[g, m], flip(me, m << low))
            )
            copies[-1].start()
        for copy in copies:
            copy.wait()
        total = slot[0]
        for m in range(1, 1 << count):
            total = total + slot[m]
        sums[...] = total

    entries = comps * panels * devices
    step_row = sums[0:1, 0:loads] / entries / (sums[1:2, 0:loads] / entries + 1e-06)
    step_ref[...] = step_row
    step = as_column(step_row)

    def update(b, carry):
        cols = pl.ds(pl.multiple_of(b * size, size), size)
        normal = trac[0, :, cols] - step * res[0, :, cols]
        slide_a = trac[1, :, cols] - step * res[1, :, cols]
        slide_b = trac[2, :, cols] - step * res[2, :, cols]
        mu = gs[comps : comps + 1, cols]
        live = gs[comps + 1 : comps + 2, cols]
        slip = jnp.sqrt(slide_a * slide_a + slide_b * slide_b + SLIP_EPS)
        stick = slip <= mu * normal
        pressed = jnp.where(stick, normal, jnp.maximum((normal + mu * slip) / (1.0 + mu * mu), 0.0))
        factor = jnp.where(stick, jnp.ones_like(slip), mu * pressed / slip)
        trac[0, :, cols] = pressed * live
        trac[1, :, cols] = factor * slide_a * live
        trac[2, :, cols] = factor * slide_b * live
        return carry

    lax.fori_loop(0, blocks, update, 0)
    outs = [pltpu.make_async_copy(trac.at[c], new_h.at[c], out_sem.at[1, c]) for c in range(comps)]
    for copy in outs:
        copy.start()
    for a in range(2):
        for c in range(comps):

            @pl.when(has_onward)
            def _():
                y_copy(a, c).wait_send()

    for c in range(comps):
        pltpu.make_async_copy(res.at[c], res_h.at[c], out_sem.at[0, c]).wait()
        outs[c].wait()


def body(wide, narrow, traction, near_kernel, neighbours, far_basis, surface_gap, friction, flags, order, approach):
    comps, loads, panels = traction.shape
    blocks, near, size = near_kernel.shape[:3]
    levels, _, rank = far_basis.shape
    cfg = (comps, loads, panels, blocks, near, size, levels, rank, wide, narrow)
    low = jnp.bfloat16
    lower = narrow.bit_length() - 1
    ranks = lambda s: pltpu.VMEM((2, comps, loads, (levels - s) * rank), low)
    dma = pltpu.SemaphoreType.DMA
    vmem = pl.BlockSpec(memory_space=pltpu.VMEM)
    anywhere = pl.BlockSpec(memory_space=pl.ANY)
    scratch = [
        pltpu.VMEM(traction.shape, jnp.float32),
        pltpu.VMEM(near_kernel.shape, low),
        pltpu.VMEM((panels, levels * rank), low),
        pltpu.VMEM(traction.shape, jnp.float32),
        pltpu.VMEM((8, panels), jnp.float32),
        pltpu.VMEM((8, panels), jnp.float32),
        pltpu.VMEM((comps, loads, levels * rank), low),
        pltpu.VMEM((comps, loads, levels * rank), jnp.float32),
        pltpu.VMEM((8, 128), jnp.float32),
        pltpu.VMEM(surface_gap.shape, jnp.float32),
        pltpu.VMEM((panels,), jnp.float32),
        pltpu.VMEM((panels,), jnp.int32),
        pltpu.VMEM((panels,), jnp.int32),
        pltpu.VMEM(approach.shape, jnp.float32),
    ]
    scratch += [pltpu.VMEM((3 * blocks, loads, size), low) for _ in range(2 * comps)]
    scratch += [ranks(s) for s in range(lower + 1)] + [ranks(s) for s in range(lower)]
    scratch += [ranks(lower + m.bit_length() - 1) for m in range(1, wide)]
    scratch += [pltpu.VMEM((count, 8, 128), jnp.float32) for count in (narrow, wide)]
    scratch += [dma((comps + levels + 6,)), dma((2, comps))]
    scratch += [dma((2, comps, lower))] * 2 + [dma((2, comps, wide))] * 2 + [dma((2, comps))] * 4
    scratch += [dma((2, max(narrow, wide)))] * 2
    new, residual, step = pl.pallas_call(
        functools.partial(kernel, cfg),
        out_shape=(
            jax.ShapeDtypeStruct(traction.shape, jnp.float32),
            jax.ShapeDtypeStruct(traction.shape, jnp.float32),
            jax.ShapeDtypeStruct((1, loads), jnp.float32),
        ),
        in_specs=[pl.BlockSpec(memory_space=pltpu.SMEM)] + [anywhere] * 8,
        out_specs=(anywhere, anywhere, vmem),
        scratch_shapes=scratch,
        compiler_params=pltpu.CompilerParams(
            collective_id=0, has_side_effects=True, vmem_limit_bytes=50 * 1024 * 1024
        ),
    )(
        neighbours,
        traction,
        near_kernel,
        far_basis,
        surface_gap,
        friction,
        flags,
        order,
        approach,
    )
    return new, residual, step.reshape(loads)


def solution(mesh):
    sizes = mesh.shape
    return jax.shard_map(
        functools.partial(body, sizes["wide"], sizes["narrow"]),
        mesh=mesh,
        in_specs=(
            P(None, None, ("wide", "narrow")),
            P(("wide", "narrow"), None, None, None),
            P(("wide", "narrow"), None),
            P(None, ("wide", "narrow"), None),
            P(None, ("wide", "narrow")),
            P(("wide", "narrow")),
            P(("wide", "narrow")),
            P(("wide", "narrow")),
            P(),
        ),
        out_specs=(P(None, None, ("wide", "narrow")), P(None, None, ("wide", "narrow")), P()),
        check_vma=False,
    )
```

```python
import functools
import math

import jax
import jax.numpy as jnp
from jax import lax
from jax.experimental import pallas as pl
from jax.experimental.pallas import tpu as pltpu
from jax.sharding import PartitionSpec as P

SLIP_EPS = 0.01
MESH = pl.DeviceIdType.MESH


def dot(a, b):
    return lax.dot_general(a, b, (((1,), (0,)), ((), ())), preferred_element_type=jnp.float32)


def dot_t(a, b):
    return lax.dot_general(a, b, (((1,), (1,)), ((), ())), preferred_element_type=jnp.float32)


def flip(me, mask):
    peer = me
    bit = 1
    while bit <= mask:
        if mask & bit:
            peer = peer + bit - 2 * bit * ((me // bit) % 2)
        bit *= 2
    return peer


def event_order(chunks, stages):
    step, lead, first, later, ahead = 4.0, 12.0, 2.0, 3.0, 5.0
    events = []
    for a in range(2):
        for c in range(chunks):
            start = a * (lead + 3.2) + c * step
            for s in range(stages):
                events.append((start + first + later * s, "tree", a, c, s))
            events.append((start + lead - 0.1, "upper", a, c, 0))
            events.append((start + ahead, "forward", a, c, 0))
            events.append((start + lead, "finish", a, c, 0))
    return [event[1:] for event in sorted(events, key=lambda event: event[0])]


def kernel(cfg, *refs):
    comps, loads, panels, blocks, near, size, levels, rank, wide, narrow = cfg
    refs = list(refs)
    take = lambda count: [refs.pop(0) for _ in range(count)]
    nb, trac_h, near_h, far_h, gap, fric, flags, order, approach = take(9)
    new_h, res_h, step_ref = take(3)
    trac, kv, bcat, res, table, gs, coef, acc, sums = take(9)
    gap_v, fric_v, flags_v, order_v, approach_v = take(5)
    halos = [take(comps) for _ in range(2)]
    devices = wide * narrow
    lower = narrow.bit_length() - 1
    sends, recvs = take(lower + 1), take(lower)
    upper_in = [None] + take(wide - 1)
    groups = [(0, lower), (lower, levels - lower)]
    slots = take(len(groups))
    load_sem, out_sem, tree_ss, tree_rs, up_ss, up_rs, x_ss, x_rs, y_ss, y_rs, stat_ss, stat_rs = take(12)

    me = lax.axis_index("wide") * narrow + lax.axis_index("narrow")
    odd = me % 2
    pair = flip(me, 1)
    onward = me + 2 - 4 * odd
    source = me - 2 + 4 * odd
    has_onward = (onward >= 0) & (onward < devices)
    has_source = (source >= 0) & (source < devices)

    def coords(peer):
        return (peer // narrow, peer % narrow)

    def remote(src, dst, ss, rs, peer):
        return pltpu.make_async_remote_copy(
            src_ref=src, dst_ref=dst, send_sem=ss, recv_sem=rs, device_id=coords(peer), device_id_type=MESH
        )

    trac_in = [pltpu.make_async_copy(trac_h.at[c], trac.at[c], load_sem.at[c]) for c in range(comps)]
    far_in = [
        pltpu.make_async_copy(far_h.at[m], bcat.at[:, m * rank : (m + 1) * rank], load_sem.at[comps + m])
        for m in range(levels)
    ]
    near_in = pltpu.make_async_copy(near_h, kv, load_sem.at[comps + levels])
    small_in = [
        pltpu.make_async_copy(src, dst, load_sem.at[comps + levels + 1 + i])
        for i, (src, dst) in enumerate(
            [(gap, gap_v), (fric, fric_v), (flags, flags_v), (order, order_v), (approach, approach_v)]
        )
    ]
    for copy in trac_in + far_in + small_in:
        copy.start()

    masks = set()
    for low, count in groups:
        masks |= set(m << low for m in range(1, 1 << count))
    barrier = pltpu.get_barrier_semaphore()
    for mask in sorted(masks):
        pl.semaphore_signal(barrier, inc=1, device_id=coords(flip(me, mask)), device_id_type=MESH)

    @pl.when(has_onward)
    def _():
        pl.semaphore_signal(barrier, inc=1, device_id=coords(onward), device_id_type=MESH)

    @pl.when(has_source)
    def _():
        pl.semaphore_signal(barrier, inc=1, device_id=coords(source), device_id_type=MESH)

    for a in range(2):
        for c in range(comps):

            @pl.when(me == 0)
            def _():
                halos[a][c][0:blocks] = jnp.zeros((blocks, loads, size), jnp.bfloat16)

            @pl.when(me == devices - 1)
            def _():
                halos[a][c][2 * blocks : 3 * blocks] = jnp.zeros((blocks, loads, size), jnp.bfloat16)

    for c in range(comps):
        trac_in[c].wait()
        for b in range(blocks):
            halos[0][c][blocks + b] = trac[c, :, b * size : (b + 1) * size].astype(jnp.bfloat16)
    for copy in far_in:
        copy.wait()
    near_in.start()

    def tree_copy(a, c, s):
        return remote(
            sends[s].at[a, c], recvs[s].at[a, c], tree_ss.at[a, c, s], tree_rs.at[a, c, s], flip(me, 1 << s)
        )

    def upper_copy(a, c, m):
        skip = (m.bit_length() - 1) * rank
        return remote(
            sends[lower].at[a, c, :, skip:],
            upper_in[m].at[a, c],
            up_ss.at[a, c, m],
            up_rs.at[a, c, m],
            flip(me, m << lower),
        )

    def x_copy(a, c):
        halo = halos[a][c]
        return remote(
            halo.at[pl.ds(blocks, blocks)],
            halo.at[pl.ds((1 - odd) * 0 + odd * 2 * blocks, blocks)],
            x_ss.at[a, c],
            x_rs.at[a, c],
            pair,
        )

    def y_copy(a, c):
        halo = halos[a][c]
        return remote(
            halo.at[pl.ds((1 - odd) * 2 * blocks, blocks)],
            halo.at[pl.ds(odd * 2 * blocks, blocks)],
            y_ss.at[a, c],
            y_rs.at[a, c],
            onward,
        )

    def project(a, c):
        total = dot(halos[a][c][blocks], bcat[0:size, :])
        for b in range(1, blocks):
            total = total + dot(halos[a][c][blocks + b], bcat[b * size : (b + 1) * size, :])
        acc[c] = total
        sends[0][a, c] = total.astype(jnp.bfloat16)

    def launch(a, c):
        tree_copy(a, c, 0).start()
        x_copy(a, c).start()

    for c in range(comps):
        project(0, c)
        if c == 0:
            pl.semaphore_wait(
                barrier, len(masks) + jnp.where(has_onward, 1, 0) + jnp.where(has_source, 1, 0)
            )
        launch(0, c)

    table[...] = jnp.zeros_like(table)
    for copy in small_in:
        copy.wait()
    table[0:comps] = gap_v[...]
    table[comps : comps + 1] = fric_v[...].reshape(1, panels)
    table[comps + 1 : comps + 2] = flags_v[...].reshape(1, panels).astype(jnp.float32)
    whole = table[...]
    high = whole.astype(jnp.bfloat16).astype(jnp.float32)
    rest = whole - high
    middle = rest.astype(jnp.bfloat16).astype(jnp.float32)
    parts = jnp.concatenate([high, middle, rest - middle, jnp.zeros_like(whole)], axis=0).astype(jnp.bfloat16)

    def gather(b, carry):
        cols = pl.ds(pl.multiple_of(b * size, size), size)
        wanted = order_v[cols].reshape(1, size) - me * panels
        chosen = lax.broadcasted_iota(jnp.int32, (panels, size), 0) == wanted
        picked = dot(parts, chosen.astype(jnp.float32).astype(jnp.bfloat16))
        rows = whole.shape[0]
        gs[:, cols] = picked[0:rows] + picked[rows : 2 * rows] + picked[2 * rows : 3 * rows]
        return carry

    lax.fori_loop(0, blocks, gather, 0)

    diagonal = lax.broadcasted_iota(jnp.int32, (loads, loads), 0) == lax.broadcasted_iota(
        jnp.int32, (loads, loads), 1
    )

    def as_column(row):
        return jnp.sum(jnp.where(diagonal, row, 0.0), axis=1, keepdims=True)

    def as_row(column):
        return jnp.sum(jnp.where(diagonal, column, 0.0), axis=0, keepdims=True)

    columns = [as_column(approach_v[c : c + 1, :]) for c in range(comps)]
    near_in.wait()

    def tree(a, c, s):
        tree_copy(a, c, s).wait()
        merged = acc[c, :, s * rank :] + recvs[s][a, c].astype(jnp.float32)
        gain = 0.64 / math.sqrt(rank * panels * 2 ** (s + 1))
        coef[c, :, s * rank : (s + 1) * rank] = (merged[:, 0:rank] * gain).astype(jnp.bfloat16)
        acc[c, :, (s + 1) * rank :] = merged[:, rank:]
        sends[s + 1][a, c] = merged[:, rank:].astype(jnp.bfloat16)
        if s + 1 < lower:
            tree_copy(a, c, s + 1).start()
        else:
            for m in reversed(range(1, wide)):
                upper_copy(a, c, m).start()

    def upper(a, c):
        total = acc[c, :, lower * rank :]
        for u in range(levels - lower):
            extra = None
            for m in range(1 << u, 2 << u):
                upper_copy(a, c, m).wait()
                piece = upper_in[m][a, c].astype(jnp.float32)
                extra = piece if extra is None else extra + piece
            total = total + extra
            gain = 0.64 / math.sqrt(rank * panels * 2 ** (lower + u + 1))
            at = (lower + u) * rank
            coef[c, :, at : at + rank] = (total[:, 0:rank] * gain).astype(jnp.bfloat16)
            total = total[:, rank:]

    def forward(a, c):
        x_copy(a, c).wait()

        @pl.when(has_onward)
        def _():
            y_copy(a, c).start()

    def finish(a, c):
        @pl.when(has_source)
        def _():
            y_copy(a, c).wait_recv()

        halo = halos[a][c]

        def block(b, carry):
            cols = pl.ds(pl.multiple_of(b * size, size), size)
            total = dot_t(coef[c], bcat[cols, :])
            for k in range(near):
                slot = nb[b, k] - nb[b, 0] + b + blocks
                total = total + dot_t(halo[slot], kv[b, k])
            if a == 0:
                value = total - (columns[c] - gs[c : c + 1, cols])
                res[c, :, cols] = value
                halos[1][c][blocks + b] = value.astype(jnp.bfloat16)
                return carry
            cross, square = carry
            cross = cross + jnp.sum(res[c, :, cols] * total, axis=1, keepdims=True)
            return cross, square + jnp.sum(total * total, axis=1, keepdims=True)

        if a == 0:
            lax.fori_loop(0, blocks, block, 0)
            project(1, c)
            launch(1, c)
            pltpu.make_async_copy(res.at[c], res_h.at[c], out_sem.at[0, c]).start()
            return None
        zero = jnp.zeros((loads, 1), jnp.float32)
        return lax.fori_loop(0, blocks, block, (zero, zero))

    cross = square = None
    for kind, a, c, s in event_order(comps, lower):
        if kind == "tree":
            tree(a, c, s)
        elif kind == "upper":
            upper(a, c)
        elif kind == "forward":
            forward(a, c)
        else:
            part = finish(a, c)
            if a == 1:
                cross = part[0] if cross is None else cross + part[0]
                square = part[1] if square is None else square + part[1]

    sums[...] = jnp.zeros_like(sums)
    sums[0:1, 0:loads] = as_row(cross)
    sums[1:2, 0:loads] = as_row(square)
    for g, (low, count) in enumerate(groups):
        slot = slots[g]
        mine = (me // (1 << low)) % (1 << count)
        slot[mine] = sums[...]
        copies = []
        for m in range(1, 1 << count):
            copies.append(
                remote(slot.at[mine], slot.at[mine], stat_ss.at[g, m], stat_rs.at[g, m], flip(me, m << low))
            )
            copies[-1].start()
        for copy in copies:
            copy.wait()
        total = slot[0]
        for m in range(1, 1 << count):
            total = total + slot[m]
        sums[...] = total

    entries = comps * panels * devices
    step_row = sums[0:1, 0:loads] / entries / (sums[1:2, 0:loads] / entries + 1e-06)
    step_ref[...] = step_row
    step = as_column(step_row)

    def update(b, carry):
        cols = pl.ds(pl.multiple_of(b * size, size), size)
        normal = trac[0, :, cols] - step * res[0, :, cols]
        slide_a = trac[1, :, cols] - step * res[1, :, cols]
        slide_b = trac[2, :, cols] - step * res[2, :, cols]
        mu = gs[comps : comps + 1, cols]
        live = gs[comps + 1 : comps + 2, cols]
        slip = jnp.sqrt(slide_a * slide_a + slide_b * slide_b + SLIP_EPS)
        stick = slip <= mu * normal
        pressed = jnp.where(stick, normal, jnp.maximum((normal + mu * slip) / (1.0 + mu * mu), 0.0))
        factor = jnp.where(stick, jnp.ones_like(slip), mu * pressed / slip)
        trac[0, :, cols] = pressed * live
        trac[1, :, cols] = factor * slide_a * live
        trac[2, :, cols] = factor * slide_b * live
        return carry

    lax.fori_loop(0, blocks, update, 0)
    outs = [pltpu.make_async_copy(trac.at[c], new_h.at[c], out_sem.at[1, c]) for c in range(comps)]
    for copy in outs:
        copy.start()
    for a in range(2):
        for c in range(comps):

            @pl.when(has_onward)
            def _():
                y_copy(a, c).wait_send()

    for c in range(comps):
        pltpu.make_async_copy(res.at[c], res_h.at[c], out_sem.at[0, c]).wait()
        outs[c].wait()


def body(wide, narrow, traction, near_kernel, neighbours, far_basis, surface_gap, friction, flags, order, approach):
    comps, loads, panels = traction.shape
    blocks, near, size = near_kernel.shape[:3]
    levels, _, rank = far_basis.shape
    cfg = (comps, loads, panels, blocks, near, size, levels, rank, wide, narrow)
    low = jnp.bfloat16
    lower = narrow.bit_length() - 1
    ranks = lambda s: pltpu.VMEM((2, comps, loads, (levels - s) * rank), low)
    dma = pltpu.SemaphoreType.DMA
    vmem = pl.BlockSpec(memory_space=pltpu.VMEM)
    anywhere = pl.BlockSpec(memory_space=pl.ANY)
    scratch = [
        pltpu.VMEM(traction.shape, jnp.float32),
        pltpu.VMEM(near_kernel.shape, low),
        pltpu.VMEM((panels, levels * rank), low),
        pltpu.VMEM(traction.shape, jnp.float32),
        pltpu.VMEM((8, panels), jnp.float32),
        pltpu.VMEM((8, panels), jnp.float32),
        pltpu.VMEM((comps, loads, levels * rank), low),
        pltpu.VMEM((comps, loads, levels * rank), jnp.float32),
        pltpu.VMEM((8, 128), jnp.float32),
        pltpu.VMEM(surface_gap.shape, jnp.float32),
        pltpu.VMEM((panels,), jnp.float32),
        pltpu.VMEM((panels,), jnp.int32),
        pltpu.VMEM((panels,), jnp.int32),
        pltpu.VMEM(approach.shape, jnp.float32),
    ]
    scratch += [pltpu.VMEM((3 * blocks, loads, size), low) for _ in range(2 * comps)]
    scratch += [ranks(s) for s in range(lower + 1)] + [ranks(s) for s in range(lower)]
    scratch += [ranks(lower + m.bit_length() - 1) for m in range(1, wide)]
    scratch += [pltpu.VMEM((count, 8, 128), jnp.float32) for count in (narrow, wide)]
    scratch += [dma((comps + levels + 6,)), dma((2, comps))]
    scratch += [dma((2, comps, lower))] * 2 + [dma((2, comps, wide))] * 2 + [dma((2, comps))] * 4
    scratch += [dma((2, max(narrow, wide)))] * 2
    new, residual, step = pl.pallas_call(
        functools.partial(kernel, cfg),
        out_shape=(
            jax.ShapeDtypeStruct(traction.shape, jnp.float32),
            jax.ShapeDtypeStruct(traction.shape, jnp.float32),
            jax.ShapeDtypeStruct((1, loads), jnp.float32),
        ),
        in_specs=[pl.BlockSpec(memory_space=pltpu.SMEM)] + [anywhere] * 8,
        out_specs=(anywhere, anywhere, vmem),
        scratch_shapes=scratch,
        compiler_params=pltpu.CompilerParams(
            collective_id=0, has_side_effects=True, vmem_limit_bytes=50 * 1024 * 1024
        ),
    )(
        neighbours,
        traction,
        near_kernel,
        far_basis,
        surface_gap,
        friction,
        flags,
        order,
        approach,
    )
    return new, residual, step.reshape(loads)


def solution(mesh):
    sizes = mesh.shape
    return jax.shard_map(
        functools.partial(body, sizes["wide"], sizes["narrow"]),
        mesh=mesh,
        in_specs=(
            P(None, None, ("wide", "narrow")),
            P(("wide", "narrow"), None, None, None),
            P(("wide", "narrow"), None),
            P(None, ("wide", "narrow"), None),
            P(None, ("wide", "narrow")),
            P(("wide", "narrow")),
            P(("wide", "narrow")),
            P(("wide", "narrow")),
            P(),
        ),
        out_specs=(P(None, None, ("wide", "narrow")), P(None, None, ("wide", "narrow")), P()),
        check_vma=False,
    )
```
